32 devices in a mesh: gx: 4 (over z), gy: 2 (over x), gz: 4 (over y, core).
Axes of the slice: x: 2, y: 2, z: 4, core: 2. Of those that a mesh axis runs over, the one named last changes fastest.
Arguments:
- block_x: float32 [16, 24, 12, 512], P(None, 'gz', 'gy', 'gx')
- block_hx: float32 [16, 24, 12, 512], P(None, 'gz', 'gy', 'gx')
- block_p: float32 [16, 24, 12, 512], P(None, 'gz', 'gy', 'gx')
- block_hp: float32 [16, 24, 12, 512], P(None, 'gz', 'gy', 'gx')
- potential: float32 [24, 12, 512], P('gz', 'gy', 'gx'), may hold values from -2 to 2
- projectors: float32 [4, 2, 4, 8, 4, 256], P('gz', 'gy', 'gx'), may hold values from -0.75 to 0.75
- coupling: float32 [4, 2, 4, 8, 4, 4], P('gz', 'gy', 'gx'), may hold values from 0.25 to 1.25
- atom_count: int32 [4, 2, 4], P('gz', 'gy', 'gx'), may hold values from 0 to 8, as said below
- proj_count: int32 [4, 2, 4, 8], P('gz', 'gy', 'gx'), may hold values from 1 to 4
- offsets: int32 [3, 4, 2, 4, 8], P(None, 'gz', 'gy', 'gx'), may hold values from 0 to 127, as said below
- extents: int32 [3, 4, 2, 4, 8], P(None, 'gz', 'gy', 'gx'), may hold values from 2 to 16, as said below
Outputs:
- w_block: float32 [16, 24, 12, 512], P(None, 'gz', 'gy', 'gx')
- hw_block: float32 [16, 24, 12, 512], P(None, 'gz', 'gy', 'gx')
- gram: float32 [48, 48], replicated
- rayleigh: float32 [48, 48], replicated
The draws below stay inside these ranges and needn't reach their ends.
Inputs may be any that keep to these rules, and one draw needn't show every extreme that they name: `atom_count`: slots at and above a domain's count are empty; some domain is full in every draw. The first proj_count projectors of a slot are used. `offsets`: components z, y, x are below 6, 6, 128. `extents`: components z, y, x are at most 4, 4, 16; some slot has the full box in every draw.
All inputs are finite; a program needn't handle non-finite values.
Results may differ from the reference program's by a relative error of at most 0.0003.
Values sent between devices are 32-bit elements; how exact they have to be, the bound alone decides.
No kernel may reach another device: no remote copies, remote signals or barrier semaphores. Data moves between devices by JAX's collectives and lax.ppermute only.
A program may use at most 64 MiB of HBM per device.

```python
import math
import jax
import jax.numpy as jnp
from jax import lax

NCOL = 16
NPROJ = 4
CZ = 6
CY = 6
CX = 128
SLOTS = 8
BZ = 4
BY = 4
BX = 16
BOXC = 256
DOMAINS_Z = 4
DOMAINS_Y = 2
DOMAINS_X = 4
NZ = 24
NY = 12
NX = 512


def paired_fields(key, salt):
    base_key = jax.random.fold_in(key, salt)
    keys = jax.random.split(base_key, 6)
    shape = (NCOL, NZ, NY, NX)
    rough = jax.random.normal(keys[1], shape, jnp.float32)
    domain_scale = jnp.exp(jax.random.uniform(keys[2], (NZ // CZ, NY // CY, 1), jnp.float32, -1.2, 1.2))
    scale_field = jnp.repeat(jnp.repeat(domain_scale, CZ, axis=0), CY, axis=1)
    first_field = rough * scale_field[None]
    mixing = jnp.diag(jax.random.uniform(keys[3], (NCOL,), jnp.float32, 1.0, 4.0)) + 0.3 * jax.random.normal(keys[4], (NCOL, NCOL), jnp.float32) / math.sqrt(NCOL)
    second_field = jnp.einsum('kzyx,kj->jzyx', first_field, mixing) + 0.5 * jax.random.normal(keys[5], shape, jnp.float32) * scale_field[None]
    return (first_field, second_field)


def draw_block_x(key, part):
    return paired_fields(key, 11)[0]


def draw_block_hx(key, part):
    return paired_fields(key, 11)[1]


def draw_block_p(key, part):
    return paired_fields(key, 23)[0]


def draw_block_hp(key, part):
    return paired_fields(key, 23)[1]


def corner_slot():
    shape = (DOMAINS_Z, DOMAINS_Y, DOMAINS_X, SLOTS)
    total_slots = DOMAINS_Z * DOMAINS_Y * DOMAINS_X * SLOTS
    flat_index = jnp.arange(total_slots, dtype=jnp.int32).reshape(shape)
    return flat_index == total_slots - SLOTS


def draw_atom_count(key, part):
    keys = jax.random.split(jax.random.fold_in(key, 5), 4)
    shape = (DOMAINS_Z, DOMAINS_Y, DOMAINS_X)
    heavy_domain = jax.random.randint(keys[0], shape, 0, 4) == 0
    large_count = jax.random.randint(keys[1], shape, SLOTS // 2, SLOTS + 1)
    small_count = jax.random.randint(keys[2], shape, 0, SLOTS // 4 + 1)
    counts = jnp.where(heavy_domain, large_count, small_count)
    domain_total = DOMAINS_Z * DOMAINS_Y * DOMAINS_X
    chosen = jax.random.randint(keys[3], (), 0, domain_total)
    flat_index = jnp.arange(domain_total, dtype=jnp.int32).reshape(shape)
    full_domain = (flat_index == chosen) | (flat_index == domain_total - 1)
    return jnp.where(full_domain, SLOTS, counts).astype(jnp.int32)


def draw_offsets(key, part):
    keys = jax.random.split(jax.random.fold_in(key, 31), 3)
    shape = (DOMAINS_Z, DOMAINS_Y, DOMAINS_X, SLOTS)
    edge_slot = corner_slot()
    along_z = jnp.where(edge_slot, CZ - 1, jax.random.randint(keys[0], shape, 0, CZ))
    along_y = jnp.where(edge_slot, CY - 1, jax.random.randint(keys[1], shape, 0, CY))
    along_x = jnp.where(edge_slot, CX - 1, jax.random.randint(keys[2], shape, 0, CX))
    return jnp.stack([along_z, along_y, along_x]).astype(jnp.int32)


def draw_extents(key, part):
    keys = jax.random.split(jax.random.fold_in(key, 47), 4)
    shape = (DOMAINS_Z, DOMAINS_Y, DOMAINS_X, SLOTS)
    total_slots = DOMAINS_Z * DOMAINS_Y * DOMAINS_X * SLOTS
    chosen = jax.random.randint(keys[3], (), 0, total_slots)
    flat_index = jnp.arange(total_slots, dtype=jnp.int32).reshape(shape)
    full_box = (flat_index == chosen) | corner_slot()
    along_z = jnp.where(full_box, BZ, jax.random.randint(keys[0], shape, 2, BZ + 1))
    along_y = jnp.where(full_box, BY, jax.random.randint(keys[1], shape, 2, BY + 1))
    along_x = jnp.where(full_box, BX, jax.random.randint(keys[2], shape, 2, BX + 1))
    return jnp.stack([along_z, along_y, along_x]).astype(jnp.int32)


def place_ends(array, rng, low, top_value):
    dims = array.shape
    index_at = [jax.random.randint(jax.random.fold_in(rng, axis), (), 0, dims[axis]) for axis in range(len(dims))]
    array = array.at[tuple(index_at)].set(low)
    longest = dims.index(max(dims))
    index_at[longest] = (index_at[longest] + 1) % dims[longest]
    return array.at[tuple(index_at)].set(top_value)


def block_levels(own_key, extent, cuts, low, largest):
    gain, own = 1.0, jax.random.fold_in(own_key, 6)
    for axis_at, blocks in cuts:
        heights = jnp.exp(jax.random.uniform(jax.random.fold_in(own, axis_at), (blocks,), jnp.float32, low / len(cuts), largest / len(cuts)))
        gain = gain * jnp.repeat(heights, extent[axis_at] // blocks).reshape([-1 if axis == axis_at else 1 for axis in range(len(extent))])
    return gain


def gaussian(stream_key, dims, scale, bound, pieces=(), kind=jnp.bfloat16):
    values = scale * jax.random.normal(stream_key, dims, jnp.float32)
    if pieces:
        values = values * block_levels(stream_key, dims, pieces, -0.22, 0.18)
    return jnp.clip(values, -bound, bound).astype(kind)


def setup_inputs(seed: int = 0) -> dict:
    splits = jax.random.split(jax.random.key(seed), 12)
    block_x = draw_block_x(jax.random.fold_in(splits[11], 71), 0)
    block_hx = draw_block_hx(jax.random.fold_in(splits[11], 71), 0)
    block_p = draw_block_p(jax.random.fold_in(splits[11], 71), 0)
    block_hp = draw_block_hp(jax.random.fold_in(splits[11], 71), 0)
    potential = jnp.clip(jax.random.uniform(splits[4], (NZ, NY, NX), jnp.float32, -2.0, 2.0) * block_levels(splits[4], (NZ, NY, NX), ((0, 4), (1, 2), (2, 4)), -0.4, 0.0), -2.0, 2.0)
    projectors = gaussian(splits[5], (DOMAINS_Z, DOMAINS_Y, DOMAINS_X, SLOTS, NPROJ, BOXC), 0.125, 0.75, ((0, 4), (1, 2), (2, 4)), jnp.float32)
    coupling = jnp.clip(0.25 + 1.0 * jax.random.uniform(splits[6], (DOMAINS_Z, DOMAINS_Y, DOMAINS_X, SLOTS, NPROJ, NPROJ), jnp.float32) ** block_levels(splits[6], (DOMAINS_Z, DOMAINS_Y, DOMAINS_X, SLOTS, NPROJ, NPROJ), ((0, 4), (1, 2), (2, 4)), -0.2, 0.2), 0.25, 1.25)
    atom_count = draw_atom_count(jax.random.fold_in(splits[11], 71), 0)
    proj_count = place_ends(jax.random.randint(splits[8], (DOMAINS_Z, DOMAINS_Y, DOMAINS_X, SLOTS), 1, NPROJ + 1), jax.random.fold_in(splits[8], 1), 1, NPROJ).astype(jnp.int32)
    offsets = draw_offsets(jax.random.fold_in(splits[11], 71), 0)
    extents = draw_extents(jax.random.fold_in(splits[11], 71), 0)
    return {"block_x": block_x, "block_hx": block_hx, "block_p": block_p, "block_hp": block_hp, "potential": potential, "projectors": projectors, "coupling": coupling, "atom_count": atom_count, "proj_count": proj_count, "offsets": offsets, "extents": extents}


LAP_CENTER = -5369.0 / 1800.0
LAP_COEFFS = (12.0 / 7.0, -15.0 / 56.0, 10.0 / 189.0, -1.0 / 112.0, 2.0 / 1925.0, -1.0 / 16632.0)
HIGHEST = lax.Precision.HIGHEST

def masked_projectors(projectors, atom_count, proj_count, extents):
    slot_index = jnp.arange(projectors.shape[-3], dtype=jnp.int32)
    live_slot = slot_index < atom_count[..., None]
    proj_index = jnp.arange(projectors.shape[-2], dtype=jnp.int32)
    live_proj = proj_index < proj_count[..., None]
    cell_index = jnp.arange(projectors.shape[-1], dtype=jnp.int32)
    along_z = cell_index // (BY * BX)
    along_y = cell_index // BX % BY
    along_x = cell_index % BX
    inside = (along_z < extents[0][..., None]) & (along_y < extents[1][..., None]) & (along_x < extents[2][..., None])
    keeper = live_slot[..., None, None] & live_proj[..., None] & inside[..., None, :]
    return jnp.where(keeper, projectors, jnp.zeros_like(projectors))

def kinetic_term(column_block):
    summed = 3.0 * LAP_CENTER * column_block
    for distance, weight in enumerate(LAP_COEFFS, start=1):
        for axis_number in (1, 2, 3):
            summed = summed + weight * (jnp.roll(column_block, distance, axis_number) + jnp.roll(column_block, -distance, axis_number))
    return -0.5 * summed

def nonlocal_term(column_block, beta_masked, sym_coupling, offsets):
    columns = column_block.shape[0]
    start_z = jnp.arange(DOMAINS_Z, dtype=jnp.int32)[:, None, None, None] * CZ + offsets[0]
    start_y = jnp.arange(DOMAINS_Y, dtype=jnp.int32)[None, :, None, None] * CY + offsets[1]
    start_x = jnp.arange(DOMAINS_X, dtype=jnp.int32)[None, None, :, None] * CX + offsets[2]
    cell_index = jnp.arange(BZ * BY * BX, dtype=jnp.int32)
    grid_z = (start_z[..., None] + cell_index // (BY * BX)) % NZ
    grid_y = (start_y[..., None] + cell_index // BX % BY) % NY
    grid_x = (start_x[..., None] + cell_index % BX) % NX
    flat_index = ((grid_z * NY + grid_y) * NX + grid_x).astype(jnp.int32)
    flat_block = column_block.reshape(columns, NZ * NY * NX)
    gathered = flat_block[:, flat_index]
    correlations = jnp.einsum('abcspk,nabcsk->abcspn', beta_masked, gathered, precision=HIGHEST)
    weights_out = jnp.einsum('abcspq,abcsqn->abcspn', sym_coupling, correlations, precision=HIGHEST)
    spread = jnp.einsum('abcspk,abcspn->nabcsk', beta_masked, weights_out, precision=HIGHEST)
    result = jnp.zeros_like(flat_block).at[:, flat_index.reshape(-1)].add(spread.reshape(columns, -1))
    return result.reshape(column_block.shape)

def inner_product(left_block, right_block, cell_weight):
    left_flat = left_block.reshape(left_block.shape[0], -1)
    right_flat = right_block.reshape(right_block.shape[0], -1)
    return jnp.einsum('ic,jc->ij', left_flat, right_flat, precision=HIGHEST) * cell_weight

def reference(block_x, block_hx, block_p, block_hp, potential, projectors, coupling, atom_count, proj_count, offsets, extents):
    cell_weight = 1.0 / (NZ * NY * NX)
    beta_masked = masked_projectors(projectors, atom_count, proj_count, extents)
    sym_coupling = 0.5 * (coupling + jnp.swapaxes(coupling, -1, -2))
    correlation = inner_product(block_x, block_x, cell_weight)
    projected = inner_product(block_x, block_hx, cell_weight)
    factor = jnp.linalg.cholesky(correlation)
    ritz_theta = jax.scipy.linalg.cho_solve((factor, True), projected)
    residual = block_hx - jnp.einsum('kzyx,kj->jzyx', block_x, ritz_theta, precision=HIGHEST)
    w_block = residual / (1.0 + potential * potential)
    hw_block = kinetic_term(w_block) + potential * w_block + nonlocal_term(w_block, beta_masked, sym_coupling, offsets)
    search_space = (block_x, w_block, block_p)
    images = (block_hx, hw_block, block_hp)
    gram = jnp.concatenate([jnp.concatenate([inner_product(left_block, right_block, cell_weight) for right_block in search_space], axis=1) for left_block in search_space], axis=0)
    rayleigh = jnp.concatenate([jnp.concatenate([inner_product(left_block, right_block, cell_weight) for right_block in images], axis=1) for left_block in search_space], axis=0)
    return (w_block, hw_block, gram, rayleigh)
```

```python
import functools
import jax
import jax.numpy as jnp
import numpy as np
from jax import lax
from jax.experimental import pallas as pl
from jax.experimental.pallas import tpu as pltpu
from jax.sharding import PartitionSpec as P

BZ = 4
BY = 4
BX = 16

LAP_CENTER = -5369.0 / 1800.0
LAP_COEFFS = (12.0 / 7.0, -15.0 / 56.0, 10.0 / 189.0, -1.0 / 112.0, 2.0 / 1925.0, -1.0 / 16632.0)
REACH = len(LAP_COEFFS)
HIGHEST = lax.Precision.HIGHEST
INTERPRET = False


def shifted(value, axis, steps):
    count = lax.axis_size(axis)
    pairs = [(source, (source + steps) % count) for source in range(count)]
    return lax.ppermute(value, axis, pairs)


def both_sides(value, axis):
    below = shifted(value, axis, 1)
    if lax.axis_size(axis) == 2:
        return below, below
    return below, shifted(value, axis, -1)


def all_sum(value, axes):
    for axis in axes:
        count = lax.axis_size(axis)
        if count & (count - 1):
            value = lax.psum(value, axis)
            continue
        step = 1
        while step < count:
            value = value + lax.ppermute(value, axis, [(i, i ^ step) for i in range(count)])
            step *= 2
    return value


def masked_projectors(projectors, atom_count, proj_count, extents):
    slot_index = jnp.arange(projectors.shape[-3], dtype=jnp.int32)
    live_slot = slot_index < atom_count[..., None]
    proj_index = jnp.arange(projectors.shape[-2], dtype=jnp.int32)
    live_proj = proj_index < proj_count[..., None]
    cell_index = jnp.arange(projectors.shape[-1], dtype=jnp.int32)
    along_z = cell_index // (BY * BX)
    along_y = cell_index // BX % BY
    along_x = cell_index % BX
    inside = (
        (along_z < extents[0][..., None])
        & (along_y < extents[1][..., None])
        & (along_x < extents[2][..., None])
    )
    keeper = live_slot[..., None, None] & live_proj[..., None] & inside[..., None, :]
    return jnp.where(keeper, projectors, jnp.zeros_like(projectors))


def band_matrices(size_x):
    cells = np.arange(size_x)
    full = dict(enumerate(LAP_COEFFS, start=1))
    full[0] = 3.0 * LAP_CENTER

    def weights(rows):
        gap = np.abs(rows[:, None] - cells[None, :])
        out = np.zeros(gap.shape, np.float32)
        for distance, weight in full.items():
            out[gap == distance] = -0.5 * weight
        return out

    inner = weights(cells)
    pad = np.zeros((8 - REACH, size_x), np.float32)
    low = np.concatenate([weights(np.arange(-REACH, 0)), pad])
    high = np.concatenate([weights(np.arange(size_x, size_x + REACH)), pad])
    pick_last = np.zeros((8, size_x), np.float32)
    pick_first = np.zeros((8, size_x), np.float32)
    for k in range(REACH):
        pick_last[k, size_x - REACH + k] = 1.0
        pick_first[k, k] = 1.0
    return inner, np.concatenate([low, high]), pick_last, pick_first


def stencil_body(own, zlo, zhi, ylo, yhi, base, out):
    size_z, size_y = own.shape[0], own.shape[1]

    def at_z(z, y):
        if z < 0:
            return zlo[size_z + z, y]
        if z >= size_z:
            return zhi[z - size_z, y]
        return own[z, y]

    def at_y(z, y):
        if y < 0:
            return ylo[z, size_y + y]
        if y >= size_y:
            return yhi[z, y - size_y]
        return own[z, y]

    for z in range(size_z):
        for y in range(size_y):
            total = base[z, y]
            for distance, weight in enumerate(LAP_COEFFS, start=1):
                beside = (at_z(z - distance, y) + at_z(z + distance, y)) + (
                    at_y(z, y - distance) + at_y(z, y + distance)
                )
                total = total + np.float32(-0.5 * weight) * beside
            out[z, y] = total


def stencil(own, zlo, zhi, ylo, yhi, base):
    size_z, size_y, columns, size_x = own.shape
    spec = pl.BlockSpec((size_z, size_y, 8, size_x), lambda i: (0, 0, i, 0))
    return pl.pallas_call(
        stencil_body,
        grid=(columns // 8,),
        in_specs=[spec] * 6,
        out_specs=spec,
        out_shape=jax.ShapeDtypeStruct(own.shape, jnp.float32),
        interpret=INTERPRET,
    )(own, zlo, zhi, ylo, yhi, base)


def place_rows(meta, beta, rows, slot):
    size_x = rows.shape[1]
    start_x = meta[slot, 2]
    lane = lax.broadcasted_iota(jnp.int32, rows.shape, 1)
    shift = jnp.where(start_x < 0, start_x + size_x, start_x)
    gap = lane - start_x
    moved = pltpu.roll(beta[slot], shift, 1)
    rows[...] = jnp.where((gap >= 0) & (gap < BX), moved, 0.0)


def overlap_body(meta, beta, fields, out, padded, rows, *, n_proj):
    size_z, size_y = fields.shape[0], fields.shape[1]
    padded[...] = jnp.zeros(padded.shape, jnp.float32)
    padded[BZ - 1 : BZ - 1 + size_z, BY - 1 : BY - 1 + size_y] = fields[...]
    out[...] = jnp.zeros(out.shape, jnp.float32)
    lane = lax.broadcasted_iota(jnp.int32, out.shape[1:], 1)
    per_tile = out.shape[2] // n_proj

    def step(slot, carry):
        @pl.when(meta[slot, 3] > 0)
        def _():
            place_rows(meta, beta, rows, slot)
            first_z = meta[slot, 0] + (BZ - 1)
            first_y = meta[slot, 1] + (BY - 1)
            sums = [jnp.zeros(out.shape[1:], jnp.float32) for _ in range(n_proj)]
            for a in range(BZ):
                for b in range(BY):
                    part = padded[first_z + a, first_y + b]
                    for p in range(n_proj):
                        row = p * BZ * BY + a * BY + b
                        sums[p] = sums[p] + part * rows[row : row + 1, :]
            tile = slot // per_tile
            left = (slot % per_tile) * n_proj
            current = out[tile]
            for p in range(n_proj):
                current = jnp.where(
                    lane == left + p, jnp.sum(sums[p], axis=1, keepdims=True), current
                )
            out[tile] = current

        return carry

    lax.fori_loop(0, meta.shape[0], step, 0)


def overlaps(meta, beta, fields, n_proj):
    size_z, size_y, columns, size_x = fields.shape
    tiles = meta.shape[0] * n_proj // 128
    return pl.pallas_call(
        functools.partial(overlap_body, n_proj=n_proj),
        in_specs=[
            pl.BlockSpec(memory_space=pltpu.SMEM),
            pl.BlockSpec(memory_space=pltpu.VMEM),
            pl.BlockSpec(memory_space=pltpu.VMEM),
        ],
        out_specs=pl.BlockSpec(memory_space=pltpu.VMEM),
        out_shape=jax.ShapeDtypeStruct((tiles, columns, 128), jnp.float32),
        scratch_shapes=[
            pltpu.VMEM((size_z + 2 * BZ - 2, size_y + 2 * BY - 2, columns, size_x), jnp.float32),
            pltpu.VMEM((n_proj * BZ * BY, size_x), jnp.float32),
        ],
        interpret=INTERPRET,
    )(meta, beta, fields)


def finish_body(meta, beta, coefs, theta_t, fields, images, w_out, hw_out, padded, rows, *, n_proj):
    size_z, size_y, columns, size_x = w_out.shape
    padded[...] = jnp.zeros(padded.shape, jnp.float32)
    lane = lax.broadcasted_iota(jnp.int32, coefs.shape[1:], 1)
    per_tile = coefs.shape[2] // n_proj

    def step(slot, carry):
        @pl.when(meta[slot, 3] > 0)
        def _():
            place_rows(meta, beta, rows, slot)
            first_z = meta[slot, 0] + (BZ - 1)
            first_y = meta[slot, 1] + (BY - 1)
            tile = coefs[slot // per_tile]
            left = (slot % per_tile) * n_proj
            scale = [
                jnp.sum(jnp.where(lane == left + p, tile, 0.0), axis=1, keepdims=True)
                for p in range(n_proj)
            ]
            scale = [jnp.broadcast_to(s, (columns, size_x)) for s in scale]
            for a in range(BZ):
                for b in range(BY):
                    total = padded[first_z + a, first_y + b]
                    for p in range(n_proj):
                        row = p * BZ * BY + a * BY + b
                        total = total + scale[p] * rows[row : row + 1, :]
                    padded[first_z + a, first_y + b] = total

        return carry

    lax.fori_loop(0, meta.shape[0], step, 0)
    turn = theta_t[...]
    for z in range(size_z):
        for y in range(size_y):
            both = jnp.concatenate([fields[z, y, :columns], images[z, y, :columns]], axis=1)
            mixed = jnp.dot(turn, both, precision=HIGHEST, preferred_element_type=jnp.float32)
            w_out[z, y] = fields[z, y, columns:] - mixed[:, :size_x]
            hw_out[z, y] = (
                images[z, y, columns:] - mixed[:, size_x:] + padded[BZ - 1 + z, BY - 1 + y]
            )


def finish(meta, beta, coefs, theta_t, fields, images, n_proj):
    size_z, size_y, both, size_x = fields.shape
    columns = both // 2
    shape = jax.ShapeDtypeStruct((size_z, size_y, columns, size_x), jnp.float32)
    vmem = pl.BlockSpec(memory_space=pltpu.VMEM)
    return pl.pallas_call(
        functools.partial(finish_body, n_proj=n_proj),
        in_specs=[pl.BlockSpec(memory_space=pltpu.SMEM)] + [vmem] * 5,
        out_specs=[vmem, vmem],
        out_shape=[shape, shape],
        scratch_shapes=[
            pltpu.VMEM((size_z + 2 * BZ - 2, size_y + 2 * BY - 2, columns, size_x), jnp.float32),
            pltpu.VMEM((n_proj * BZ * BY, size_x), jnp.float32),
        ],
        interpret=INTERPRET,
    )(meta, beta, coefs, theta_t, fields, images)


def gather_lower(own, sizes):
    value = own[None]
    for axis, dim in (("gx", 2), ("gy", 1), ("gz", 0)):
        lower = shifted(value, axis, 1)
        move = np.zeros((own.shape[-1],), np.float32)
        move[-128 + dim] = sizes[dim]
        value = jnp.concatenate([value, lower - move], axis=0)
    return value.reshape(-1, own.shape[-1])


def per_device(
    block_x,
    block_hx,
    block_p,
    block_hp,
    potential,
    projectors,
    coupling,
    atom_count,
    proj_count,
    offsets,
    extents,
):
    columns, size_z, size_y, size_x = block_x.shape
    slots, n_proj = projectors.shape[-3], projectors.shape[-2]
    cells = size_z * size_y
    cell_weight = 1.0 / (
        cells * size_x * lax.axis_size("gx") * lax.axis_size("gy") * lax.axis_size("gz")
    )
    beta_masked = masked_projectors(projectors, atom_count, proj_count, extents)[0, 0, 0]
    sym_coupling = (0.5 * (coupling + jnp.swapaxes(coupling, -1, -2)))[0, 0, 0]
    live = jnp.arange(slots, dtype=jnp.int32) < atom_count[0, 0, 0]
    ints = jnp.concatenate([offsets[:, 0, 0, 0], extents[:, 0, 0, 0], live[None].astype(jnp.int32)])
    tail = jnp.pad(ints.T.astype(jnp.float32), ((0, 0), (0, 128 - ints.shape[0])))
    packed = jnp.concatenate([beta_masked.reshape(slots, -1), tail], axis=1)
    near = gather_lower(packed, (size_z, size_y, size_x))
    beta_near = near[:, :-128].reshape(-1, n_proj * BZ * BY, BX)
    beta_near = jnp.pad(beta_near, ((0, 0), (0, 0), (0, size_x - BX)))
    facts = near[:, -128:].astype(jnp.int32)
    reaches = jnp.all(facts[:, 0:3] + facts[:, 3:6] > 0, axis=1) & (facts[:, 6] > 0)
    meta = jnp.concatenate([facts[:, 0:3], reaches[:, None].astype(jnp.int32)], axis=1)

    def turned(block):
        return jnp.transpose(block, (1, 2, 0, 3))

    pot = potential[:, :, None, :]
    gain = 1.0 / (1.0 + pot * pot)
    xt, hxt, pt, hpt = turned(block_x), turned(block_hx), turned(block_p), turned(block_hp)
    fields = jnp.concatenate([xt * gain, hxt * gain], axis=2)
    wide = 2 * columns
    zlo, zhi = both_sides(fields, "gz")
    ylo, yhi = both_sides(fields, "gy")
    inner, outer, pick_last, pick_first = band_matrices(size_x)
    flat = fields.reshape(cells * wide, size_x)
    contract_last = (((1,), (1,)), ((), ()))
    last = lax.dot_general(pick_last, flat, contract_last, precision=HIGHEST)
    first = lax.dot_general(pick_first, flat, contract_last, precision=HIGHEST)
    sides = jnp.concatenate([shifted(last, "gx", 1), shifted(first, "gx", -1)], axis=0)
    base = jnp.dot(flat, inner, precision=HIGHEST)
    edge = lax.dot_general(sides, outer, (((0,), (0,)), ((), ())), precision=HIGHEST)
    base = (base + edge).reshape(fields.shape) + pot * fields

    search = jnp.concatenate([fields, xt, pt], axis=2)
    sums = functools.partial(jnp.einsum, "zycx,zydx->cd", precision=HIGHEST)
    early = sums(search, jnp.concatenate([search, hxt, hpt], axis=2))

    found = overlaps(meta, beta_near, search, n_proj)
    half = found.shape[0] // 2
    found = found[:half] + shifted(found[half:], "gz", -1)
    found = found.transpose(1, 0, 2).reshape(2 * wide, -1)
    half = found.shape[1] // 2
    found = found[:, :half] + shifted(found[:, half:], "gy", -1)
    half = found.shape[1] // 2
    found = found[:, :half] + shifted(found[:, half:], "gx", -1)
    eye = jnp.eye(slots, dtype=jnp.float32)
    spread_d = (eye[:, None, :, None] * sym_coupling[:, :, None, :]).reshape(
        slots * n_proj, slots * n_proj
    )
    weighted = jnp.dot(found[:wide], spread_d, precision=HIGHEST)
    boxes = lax.dot_general(found, weighted, contract_last, precision=HIGHEST)
    back = weighted
    for axis in ("gx", "gy"):
        back = jnp.concatenate([back, shifted(back, axis, 1)], axis=1)
    back = jnp.stack([back, shifted(back, "gz", 1)])
    back = back.reshape(2, wide, -1, 128).transpose(0, 2, 1, 3).reshape(-1, wide, 128)

    images = stencil(fields, zlo, zhi, ylo, yhi, base)
    late = sums(search, images) + boxes
    total = all_sum(jnp.concatenate([early, late], axis=1), ("gz", "gy", "gx")) * cell_weight

    c = columns
    correlation = total[2 * c : 3 * c, 2 * c : 3 * c]
    projected = total[2 * c : 3 * c, 4 * c : 5 * c]
    factor = jnp.linalg.cholesky(correlation)
    theta = jax.scipy.linalg.cho_solve((factor, True), projected)
    one = jnp.eye(c, dtype=jnp.float32)
    nil = jnp.zeros((c, c), jnp.float32)
    basis = jnp.block([[nil, -theta, nil], [nil, one, nil], [one, nil, nil], [nil, nil, one]])
    right = jnp.concatenate(
        [
            jnp.pad(basis, ((0, 0), (0, 3 * c))),
            jnp.block([[nil] * 3 + [one, nil, nil], [nil] * 3 + [nil, nil, one]]),
            jnp.block([[nil] * 4 + [-theta, nil], [nil] * 4 + [one, nil]]),
        ],
        axis=0,
    )
    left = lax.dot_general(basis, total, (((0,), (0,)), ((), ())), precision=HIGHEST)
    tables = jnp.dot(left, right, precision=HIGHEST)

    theta_t = theta.T
    coefs = back[:, c:] - jnp.einsum("jk,tks->tjs", theta_t, back[:, :c], precision=HIGHEST)
    w_t, hw_t = finish(meta, beta_near, coefs, theta_t, fields, images, n_proj)
    w_block = jnp.transpose(w_t, (2, 0, 1, 3))
    hw_block = jnp.transpose(hw_t, (2, 0, 1, 3))
    return (w_block, hw_block, tables[:, : 3 * c], tables[:, 3 * c :])


def solution(mesh):
    in_specs = (
        P(None, "gz", "gy", "gx"),
        P(None, "gz", "gy", "gx"),
        P(None, "gz", "gy", "gx"),
        P(None, "gz", "gy", "gx"),
        P("gz", "gy", "gx"),
        P("gz", "gy", "gx", None, None, None),
        P("gz", "gy", "gx", None, None, None),
        P("gz", "gy", "gx"),
        P("gz", "gy", "gx", None),
        P(None, "gz", "gy", "gx", None),
        P(None, "gz", "gy", "gx", None),
    )
    out_specs = (P(None, "gz", "gy", "gx"), P(None, "gz", "gy", "gx"), P(), P())
    return jax.shard_map(
        per_device, mesh=mesh, in_specs=in_specs, out_specs=out_specs, check_vma=False
    )
```

```python
import functools
import jax
import jax.numpy as jnp
import numpy as np
from jax import lax
from jax.experimental import pallas as pl
from jax.experimental.pallas import tpu as pltpu
from jax.sharding import PartitionSpec as P

BZ = 4
BY = 4
BX = 16

LAP_CENTER = -5369.0 / 1800.0
LAP_COEFFS = (12.0 / 7.0, -15.0 / 56.0, 10.0 / 189.0, -1.0 / 112.0, 2.0 / 1925.0, -1.0 / 16632.0)
REACH = len(LAP_COEFFS)
HIGHEST = lax.Precision.HIGHEST
INTERPRET = False


def shifted(value, axis, steps):
    count = lax.axis_size(axis)
    pairs = [(source, (source + steps) % count) for source in range(count)]
    return lax.ppermute(value, axis, pairs)


def both_sides(value, axis):
    below = shifted(value, axis, 1)
    if lax.axis_size(axis) == 2:
        return below, below
    return below, shifted(value, axis, -1)


def all_sum(value, axes):
    for axis in axes:
        count = lax.axis_size(axis)
        if count & (count - 1):
            value = lax.psum(value, axis)
            continue
        step = 1
        while step < count:
            value = value + lax.ppermute(value, axis, [(i, i ^ step) for i in range(count)])
            step *= 2
    return value


def masked_projectors(projectors, atom_count, proj_count, extents):
    slot_index = jnp.arange(projectors.shape[-3], dtype=jnp.int32)
    live_slot = slot_index < atom_count[..., None]
    proj_index = jnp.arange(projectors.shape[-2], dtype=jnp.int32)
    live_proj = proj_index < proj_count[..., None]
    cell_index = jnp.arange(projectors.shape[-1], dtype=jnp.int32)
    along_z = cell_index // (BY * BX)
    along_y = cell_index // BX % BY
    along_x = cell_index % BX
    inside = (
        (along_z < extents[0][..., None])
        & (along_y < extents[1][..., None])
        & (along_x < extents[2][..., None])
    )
    keeper = live_slot[..., None, None] & live_proj[..., None] & inside[..., None, :]
    return jnp.where(keeper, projectors, jnp.zeros_like(projectors))


def band_matrices(size_x):
    cells = np.arange(size_x)
    full = dict(enumerate(LAP_COEFFS, start=1))
    full[0] = 3.0 * LAP_CENTER

    def weights(rows):
        gap = np.abs(rows[:, None] - cells[None, :])
        out = np.zeros(gap.shape, np.float32)
        for distance, weight in full.items():
            out[gap == distance] = -0.5 * weight
        return out

    inner = weights(cells)
    pad = np.zeros((8 - REACH, size_x), np.float32)
    low = np.concatenate([weights(np.arange(-REACH, 0)), pad])
    high = np.concatenate([weights(np.arange(size_x, size_x + REACH)), pad])
    pick_last = np.zeros((8, size_x), np.float32)
    pick_first = np.zeros((8, size_x), np.float32)
    for k in range(REACH):
        pick_last[k, size_x - REACH + k] = 1.0
        pick_first[k, k] = 1.0
    return inner, np.concatenate([low, high]), pick_last, pick_first


def spec_of(space):
    return pl.BlockSpec(memory_space=space)


def kernel_call(body, count, out_shape, scratch_shapes=(), scalars=0):
    vmem = spec_of(pltpu.VMEM)
    many = isinstance(out_shape, (list, tuple))
    return pl.pallas_call(
        body,
        in_specs=[spec_of(pltpu.SMEM)] * scalars + [vmem] * (count - scalars),
        out_specs=[vmem] * len(out_shape) if many else vmem,
        out_shape=out_shape,
        scratch_shapes=scratch_shapes,
        interpret=INTERPRET,
    )


def floats(*shape):
    return jax.ShapeDtypeStruct(shape, jnp.float32)


def over_last(left, right):
    return lax.dot_general(
        left,
        right,
        (((1,), (1,)), ((), ())),
        precision=HIGHEST,
        preferred_element_type=jnp.float32,
    )


def prepare_body(xt, hxt, pot, fields):
    columns = xt.shape[2]
    for z in range(xt.shape[0]):
        for y in range(xt.shape[1]):
            here = pot[z, y : y + 1, :]
            gain = 1.0 / (1.0 + here * here)
            fields[z, y, :columns] = xt[z, y] * gain
            fields[z, y, columns:] = hxt[z, y] * gain


def early_body(fields, xt, pt, hxt, hpt, pot, inner, base, table):
    size_z, size_y, wide, size_x = fields.shape
    columns = wide // 2
    total = jnp.zeros((4 * columns, 6 * columns), jnp.float32)
    for z in range(size_z):
        for y in range(0, size_y, 2):
            sides = [
                jnp.concatenate(
                    [fields[z, w], xt[z, w], pt[z, w], hxt[z, w], hpt[z, w]], axis=0
                )
                for w in range(y, min(y + 2, size_y))
            ]
            both = jnp.concatenate(sides, axis=1)
            total = total + over_last(both[: 4 * columns], both)
    table[...] = jnp.zeros(table.shape, jnp.float32)
    table[:, : 6 * columns] = total
    for z in range(size_z):
        flat = fields[z].reshape(size_y * wide, size_x)
        mixed = jnp.dot(flat, inner[...], precision=HIGHEST, preferred_element_type=jnp.float32)
        for y in range(size_y):
            base[z, y] = mixed[y * wide : (y + 1) * wide] + pot[z, y : y + 1, :] * fields[z, y]


def late_body(own, zlo, zhi, ylo, yhi, base, edge, xt, pt, out, table):
    size_z, size_y, wide, size_x = own.shape
    columns = wide // 2

    def at_z(z, y, c):
        if z < 0:
            return zlo[size_z + z, y, c]
        if z >= size_z:
            return zhi[z - size_z, y, c]
        return own[z, y, c]

    def at_y(z, y, c):
        if y < 0:
            return ylo[z, size_y + y, c]
        if y >= size_y:
            return yhi[z, y - size_y, c]
        return own[z, y, c]

    result = jnp.zeros((4 * columns, wide), jnp.float32)
    for z in range(size_z):
        for first in range(0, size_y, 2):
            span = range(first, min(first + 2, size_y))
            for y in span:
                for start in range(0, wide, 8):
                    c = pl.ds(start, 8)
                    total = base[z, y, c] + edge[z, y, c]
                    for distance, weight in enumerate(LAP_COEFFS, start=1):
                        beside = (at_z(z - distance, y, c) + at_z(z + distance, y, c)) + (
                            at_y(z, y - distance, c) + at_y(z, y + distance, c)
                        )
                        total = total + np.float32(-0.5 * weight) * beside
                    out[z, y, c] = total
            left = jnp.concatenate(
                [jnp.concatenate([own[z, y], xt[z, y], pt[z, y]], axis=0) for y in span], axis=1
            )
            right = jnp.concatenate([out[z, y] for y in span], axis=1)
            result = result + over_last(left, right)
    table[...] = result


def place_rows(meta, near, rows, slot, slots):
    size_x = rows.shape[1]
    per = 128 // BX
    start_x = meta[slot, 2]
    box = near[slot // slots, pl.ds(pl.multiple_of((slot % slots) * 8, 8), 8), :]
    lane = lax.broadcasted_iota(jnp.int32, box.shape, 1)
    gap = lane - start_x
    inside = (gap >= 0) & (gap < BX)
    for k in range(per):
        shift = lax.rem(start_x - k * BX + 2 * size_x, size_x)
        rows[k * 8 : (k + 1) * 8, :] = jnp.where(inside, pltpu.roll(box, shift, 1), 0.0)


def row_of(p, a, b):
    at = (p * BZ + a) * BY + b
    per = 128 // BX
    return (at % per) * 8 + at // per


def overlap_body(meta, near, fields, xt, pt, out, padded, rows, *, n_proj, slots):
    size_z, size_y, wide = fields.shape[0], fields.shape[1], fields.shape[2]
    columns = wide // 2
    padded[...] = jnp.zeros(padded.shape, jnp.float32)
    zs, ys = slice(BZ - 1, BZ - 1 + size_z), slice(BY - 1, BY - 1 + size_y)
    padded[zs, ys, :wide] = fields[...]
    padded[zs, ys, wide : wide + columns] = xt[...]
    padded[zs, ys, wide + columns :] = pt[...]
    out[...] = jnp.zeros(out.shape, jnp.float32)
    lane = lax.broadcasted_iota(jnp.int32, out.shape[1:], 1)
    per_tile = out.shape[2] // n_proj

    def step(slot, carry):
        @pl.when(meta[slot, 3] > 0)
        def _():
            place_rows(meta, near, rows, slot, slots)
            first_z = meta[slot, 0] + (BZ - 1)
            first_y = meta[slot, 1] + (BY - 1)
            sums = [jnp.zeros(out.shape[1:], jnp.float32) for _ in range(n_proj)]
            for a in range(BZ):
                for b in range(BY):
                    part = padded[first_z + a, first_y + b]
                    for p in range(n_proj):
                        row = row_of(p, a, b)
                        sums[p] = sums[p] + part * rows[row : row + 1, :]
            tile = slot // per_tile
            left = (slot % per_tile) * n_proj
            current = out[tile]
            for p in range(n_proj):
                current = jnp.where(
                    lane == left + p, jnp.sum(sums[p], axis=1, keepdims=True), current
                )
            out[tile] = current

        return carry

    lax.fori_loop(0, meta.shape[0], step, 0)


def finish_body(
    meta, near, back, total, fixed, fields, images, w_out, hw_out, gram, ray, padded, rows, coefs,
    *, n_proj, slots
):
    size_z, size_y, columns, size_x = w_out.shape
    c = columns
    full = total[...]
    grid = full[2 * c : 3 * c]
    which = lax.broadcasted_iota(jnp.int32, grid.shape, 0)
    for k in range(c):
        line = grid[k : k + 1, :]
        line = line * (1.0 / line[:, 2 * c + k : 2 * c + k + 1])
        grid = jnp.where(which == k, line, grid - grid[:, 2 * c + k : 2 * c + k + 1] * line)
    lane = lax.broadcasted_iota(jnp.int32, grid.shape, 1)
    theta = jnp.where(lane < c, pltpu.roll(grid, 128 - 4 * c, 1), 0.0)
    square = jnp.concatenate([theta, jnp.zeros((128 - c, 128), jnp.float32)], axis=0)
    turn = jnp.transpose(square)[:c, :c]

    def mix(value):
        return jnp.dot(turn, value, precision=HIGHEST, preferred_element_type=jnp.float32)

    left = jnp.concatenate([full[2 * c : 3 * c], full[c : 2 * c] - mix(full[:c]), full[3 * c :]], axis=0)
    nil = jnp.zeros((c, 128), jnp.float32)
    moved = jnp.concatenate(
        [pltpu.roll(theta, c, 1)] + [nil] * 5 + [pltpu.roll(theta, 5 * c, 1), nil], axis=0
    )
    tables = jnp.dot(
        left, fixed[...] - moved, precision=HIGHEST, preferred_element_type=jnp.float32
    )
    gram[...] = tables[:, : 3 * c]
    ray[...] = pltpu.roll(tables, 128 - 4 * c, 1)[:, : 3 * c]

    for t in range(back.shape[0]):
        coefs[t] = back[t, c:] - mix(back[t, :c])
    padded[...] = jnp.zeros(padded.shape, jnp.float32)
    per_tile = back.shape[2] // n_proj

    def step(slot, carry):
        @pl.when(meta[slot, 3] > 0)
        def _():
            place_rows(meta, near, rows, slot, slots)
            first_z = meta[slot, 0] + (BZ - 1)
            first_y = meta[slot, 1] + (BY - 1)
            tile = coefs[slot // per_tile]
            begin = (slot % per_tile) * n_proj
            scale = [
                jnp.sum(jnp.where(lane == begin + p, tile, 0.0), axis=1, keepdims=True)
                for p in range(n_proj)
            ]
            scale = [jnp.broadcast_to(s, (columns, size_x)) for s in scale]
            for a in range(BZ):
                for b in range(BY):
                    value = padded[first_z + a, first_y + b]
                    for p in range(n_proj):
                        row = row_of(p, a, b)
                        value = value + scale[p] * rows[row : row + 1, :]
                    padded[first_z + a, first_y + b] = value

        return carry

    lax.fori_loop(0, meta.shape[0], step, 0)
    for z in range(size_z):
        for y in range(size_y):
            mixed = mix(jnp.concatenate([fields[z, y, :c], images[z, y, :c]], axis=1))
            w_out[z, y] = fields[z, y, c:] - mixed[:, :size_x]
            hw_out[z, y] = images[z, y, c:] - mixed[:, size_x:] + padded[BZ - 1 + z, BY - 1 + y]


def per_device(
    block_x,
    block_hx,
    block_p,
    block_hp,
    potential,
    projectors,
    coupling,
    atom_count,
    proj_count,
    offsets,
    extents,
):
    columns, size_z, size_y, size_x = block_x.shape
    slots, n_proj = projectors.shape[-3], projectors.shape[-2]
    cells = size_z * size_y
    c, wide = columns, 2 * columns
    cell_weight = 1.0 / (
        cells * size_x * lax.axis_size("gx") * lax.axis_size("gy") * lax.axis_size("gz")
    )
    beta_masked = masked_projectors(projectors, atom_count, proj_count, extents)[0, 0, 0]
    sym_coupling = (0.5 * (coupling + jnp.swapaxes(coupling, -1, -2)))[0, 0, 0]
    live = jnp.arange(slots, dtype=jnp.int32) < atom_count[0, 0, 0]
    ints = jnp.concatenate([offsets[:, 0, 0, 0], extents[:, 0, 0, 0], live[None].astype(jnp.int32)])
    tail = jnp.pad(ints.T.astype(jnp.float32), ((0, 0), (0, 128 - ints.shape[0])))
    near = jnp.concatenate([beta_masked.reshape(slots * 8, 128), tail], axis=0)[None]

    def add_lower(value, axis, dim, size):
        move = np.zeros((near.shape[1], 128), np.float32)
        move[slots * 8 :, dim] = size
        return jnp.concatenate([value, shifted(value, axis, 1) - move], axis=0)

    def turned(block):
        return jnp.transpose(block, (1, 2, 0, 3))

    near = add_lower(near, "gx", 2, size_x)
    xt, hxt, pt, hpt = turned(block_x), turned(block_hx), turned(block_p), turned(block_hp)
    fields = kernel_call(prepare_body, 3, floats(size_z, size_y, wide, size_x))(xt, hxt, potential)
    fields, near = lax.optimization_barrier((fields, near))
    zlo, zhi = both_sides(fields, "gz")
    ylo, yhi = both_sides(fields, "gy")
    near = add_lower(near, "gy", 1, size_y)
    inner, outer, pick_last, pick_first = band_matrices(size_x)
    picked = over_last(np.concatenate([pick_last, pick_first]), fields.reshape(-1, size_x))
    sides = jnp.concatenate([shifted(picked[:8], "gx", 1), shifted(picked[8:], "gx", -1)], axis=0)
    base, early = kernel_call(
        early_body, 7, [floats(size_z, size_y, wide, size_x), floats(4 * c, 8 * c)]
    )(fields, xt, pt, hxt, hpt, potential, inner)
    base, early, near, sides = lax.optimization_barrier((base, early, near, sides))
    near = add_lower(near, "gz", 0, size_z)
    edge = lax.dot_general(sides, outer, (((0,), (0,)), ((), ())), precision=HIGHEST)
    edge = edge.reshape(fields.shape)
    facts = near[:, slots * 8 :, :8].reshape(-1, 8).astype(jnp.int32)
    reaches = jnp.all(facts[:, 0:3] + facts[:, 3:6] > 0, axis=1) & (facts[:, 6] > 0)
    meta = jnp.concatenate([facts[:, 0:3], reaches[:, None].astype(jnp.int32)], axis=1)

    pads = (size_z + 2 * BZ - 2, size_y + 2 * BY - 2)
    rows_shape = pltpu.VMEM((n_proj * BZ * BY, size_x), jnp.float32)
    tiles = meta.shape[0] * n_proj // 128
    found = kernel_call(
        functools.partial(overlap_body, n_proj=n_proj, slots=slots),
        5,
        floats(tiles, 4 * c, 128),
        [pltpu.VMEM(pads + (4 * c, size_x), jnp.float32), rows_shape],
        scalars=1,
    )(meta, near, fields, xt, pt)
    half = tiles // 2
    found = found[:half] + shifted(found[half:], "gz", -1)
    images, late = kernel_call(
        late_body, 9, [floats(size_z, size_y, wide, size_x), floats(4 * c, wide)]
    )(fields, zlo, zhi, ylo, yhi, base, edge, xt, pt)
    images, late, found = lax.optimization_barrier((images, late, found))
    found = found.transpose(1, 0, 2).reshape(4 * c, -1)
    half = found.shape[1] // 2
    found = found[:, :half] + shifted(found[:, half:], "gy", -1)
    half = found.shape[1] // 2
    found = found[:, :half] + shifted(found[:, half:], "gx", -1)
    eye = jnp.eye(slots, dtype=jnp.float32)
    spread_d = (eye[:, None, :, None] * sym_coupling[:, :, None, :]).reshape(
        slots * n_proj, slots * n_proj
    )
    weighted = jnp.dot(found[:wide], spread_d, precision=HIGHEST)
    late = late + over_last(found, weighted)
    total = early + jnp.pad(late, ((0, 0), (6 * c, 0)))
    total = all_sum(total, ("gz", "gy", "gx")) * cell_weight
    back = weighted
    for axis in ("gx", "gy"):
        back = jnp.concatenate([back, shifted(back, axis, 1)], axis=1)
    back = jnp.stack([back, shifted(back, "gz", 1)])
    back = back.reshape(2, wide, -1, 128).transpose(0, 2, 1, 3).reshape(-1, wide, 128)

    fixed = np.zeros((8 * c, 128), np.float32)
    one = np.eye(c, dtype=np.float32)
    for group, place in ((1, 1), (2, 0), (3, 2), (4, 4), (5, 6), (7, 5)):
        fixed[group * c : (group + 1) * c, place * c : (place + 1) * c] = one
    half_shape = floats(size_z, size_y, columns, size_x)
    w_t, hw_t, gram, rayleigh = kernel_call(
        functools.partial(finish_body, n_proj=n_proj, slots=slots),
        7,
        [half_shape, half_shape, floats(3 * c, 3 * c), floats(3 * c, 3 * c)],
        [
            pltpu.VMEM(pads + (columns, size_x), jnp.float32),
            rows_shape,
            pltpu.VMEM((tiles, columns, 128), jnp.float32),
        ],
        scalars=1,
    )(meta, near, back, total, fixed, fields, images)
    w_block = jnp.transpose(w_t, (2, 0, 1, 3))
    hw_block = jnp.transpose(hw_t, (2, 0, 1, 3))
    return (w_block, hw_block, gram, rayleigh)


def solution(mesh):
    in_specs = (
        P(None, "gz", "gy", "gx"),
        P(None, "gz", "gy", "gx"),
        P(None, "gz", "gy", "gx"),
        P(None, "gz", "gy", "gx"),
        P("gz", "gy", "gx"),
        P("gz", "gy", "gx", None, None, None),
        P("gz", "gy", "gx", None, None, None),
        P("gz", "gy", "gx"),
        P("gz", "gy", "gx", None),
        P(None, "gz", "gy", "gx", None),
        P(None, "gz", "gy", "gx", None),
    )
    out_specs = (P(None, "gz", "gy", "gx"), P(None, "gz", "gy", "gx"), P(), P())
    return jax.shard_map(
        per_device, mesh=mesh, in_specs=in_specs, out_specs=out_specs, check_vma=False
    )
```

```python
import functools
import jax
import jax.numpy as jnp
import numpy as np
from jax import lax
from jax.experimental import pallas as pl
from jax.experimental.pallas import tpu as pltpu
from jax.sharding import PartitionSpec as P

BZ = 4
BY = 4
BX = 16

LAP_CENTER = -5369.0 / 1800.0
LAP_COEFFS = (12.0 / 7.0, -15.0 / 56.0, 10.0 / 189.0, -1.0 / 112.0, 2.0 / 1925.0, -1.0 / 16632.0)
REACH = len(LAP_COEFFS)
HIGHEST = lax.Precision.HIGHEST
INTERPRET = False


def shifted(value, axis, steps):
    count = lax.axis_size(axis)
    pairs = [(source, (source + steps) % count) for source in range(count)]
    return lax.ppermute(value, axis, pairs)


def both_sides(value, axis):
    below = shifted(value, axis, 1)
    if lax.axis_size(axis) == 2:
        return below, below
    return below, shifted(value, axis, -1)


def all_sum(value, axes):
    for axis in axes:
        count = lax.axis_size(axis)
        if count & (count - 1):
            value = lax.psum(value, axis)
            continue
        step = 1
        while step < count:
            value = value + lax.ppermute(value, axis, [(i, i ^ step) for i in range(count)])
            step *= 2
    return value


def band_matrices(size_x):
    cells = np.arange(size_x)
    full = dict(enumerate(LAP_COEFFS, start=1))
    full[0] = 3.0 * LAP_CENTER

    def weights(rows):
        gap = np.abs(rows[:, None] - cells[None, :])
        out = np.zeros(gap.shape, np.float32)
        for distance, weight in full.items():
            out[gap == distance] = -0.5 * weight
        return out

    inner = weights(cells)
    pad = np.zeros((8 - REACH, size_x), np.float32)
    low = np.concatenate([weights(np.arange(-REACH, 0)), pad])
    high = np.concatenate([weights(np.arange(size_x, size_x + REACH)), pad])
    pick_last = np.zeros((8, size_x), np.float32)
    pick_first = np.zeros((8, size_x), np.float32)
    for k in range(REACH):
        pick_last[k, size_x - REACH + k] = 1.0
        pick_first[k, k] = 1.0
    return inner, np.concatenate([low, high]), pick_last, pick_first


def spec_of(space):
    return pl.BlockSpec(memory_space=space)


def kernel_call(body, count, out_shape, scratch_shapes=(), scalars=0):
    vmem = spec_of(pltpu.VMEM)
    many = isinstance(out_shape, (list, tuple))
    return pl.pallas_call(
        body,
        in_specs=[spec_of(pltpu.SMEM)] * scalars + [vmem] * (count - scalars),
        out_specs=[vmem] * len(out_shape) if many else vmem,
        out_shape=out_shape,
        scratch_shapes=scratch_shapes,
        interpret=INTERPRET,
    )


def floats(*shape):
    return jax.ShapeDtypeStruct(shape, jnp.float32)


def over_last(left, right):
    return lax.dot_general(
        left,
        right,
        (((1,), (1,)), ((), ())),
        precision=HIGHEST,
        preferred_element_type=jnp.float32,
    )


def prepare_body(
    where, extent, used, count, projectors, xt, hxt, pot, picks, fields, picked, near, *, slots
):
    columns, size_x = xt.shape[2:]
    n_proj = projectors.shape[1]
    per_proj = BZ * BY * BX // 128
    line = lax.broadcasted_iota(jnp.int32, (n_proj * per_proj, 128), 0)
    lane = lax.broadcasted_iota(jnp.int32, (n_proj * per_proj, 128), 1)
    cell = line % per_proj * 128 + lane
    along_z = cell // (BY * BX)
    along_y = cell // BX % BY
    along_x = cell % BX
    owner = line // per_proj
    for slot in range(slots):
        values = jnp.concatenate(
            [
                projectors[slot, p : p + 1, h * 128 : (h + 1) * 128]
                for p in range(n_proj)
                for h in range(per_proj)
            ],
            axis=0,
        )
        keep = (
            (along_z < extent[0, slot])
            & (along_y < extent[1, slot])
            & (along_x < extent[2, slot])
            & (owner < used[slot])
            & (count[0] > slot)
        )
        near[0, slot * 8 : (slot + 1) * 8, :] = jnp.where(keep, values, 0.0)
    first = lax.broadcasted_iota(jnp.int32, (1, 128), 1)
    for slot in range(slots):
        facts = jnp.zeros((1, 128), jnp.int32)
        for d in range(3):
            facts = jnp.where(first == d, where[d, slot], facts)
            facts = jnp.where(first == 3 + d, extent[d, slot], facts)
        facts = jnp.where(first == 6, jnp.where(count[0] > slot, 1, 0), facts)
        near[0, slots * 8 + slot : slots * 8 + slot + 1, :] = facts.astype(jnp.float32)
    for z in range(xt.shape[0]):
        for y in range(xt.shape[1]):
            here = pot[z, y : y + 1, :]
            gain = 1.0 / (1.0 + here * here)
            fields[z, y, :columns] = xt[z, y] * gain
            fields[z, y, columns:] = hxt[z, y] * gain
    picked[...] = over_last(picks[...], fields[...].reshape(-1, size_x))


def early_body(fields, xt, pt, hxt, hpt, pot, inner, base, table):
    size_z, size_y, wide, size_x = fields.shape
    columns = wide // 2
    total = jnp.zeros((4 * columns, 6 * columns), jnp.float32)
    for z in range(size_z):
        for y in range(0, size_y, 2):
            sides = [
                jnp.concatenate(
                    [fields[z, w], xt[z, w], pt[z, w], hxt[z, w], hpt[z, w]], axis=0
                )
                for w in range(y, min(y + 2, size_y))
            ]
            both = jnp.concatenate(sides, axis=1)
            total = total + over_last(both[: 4 * columns], both)
    table[...] = jnp.zeros(table.shape, jnp.float32)
    table[:, : 6 * columns] = total
    for z in range(size_z):
        flat = fields[z].reshape(size_y * wide, size_x)
        mixed = jnp.dot(flat, inner[...], precision=HIGHEST, preferred_element_type=jnp.float32)
        for y in range(size_y):
            base[z, y] = mixed[y * wide : (y + 1) * wide] + pot[z, y : y + 1, :] * fields[z, y]


def late_body(own, zlo, zhi, ylo, yhi, base, edge, xt, pt, out, table):
    size_z, size_y, wide, size_x = own.shape
    columns = wide // 2

    def at_z(z, y, c):
        if z < 0:
            return zlo[size_z + z, y, c]
        if z >= size_z:
            return zhi[z - size_z, y, c]
        return own[z, y, c]

    def at_y(z, y, c):
        if y < 0:
            return ylo[z, size_y + y, c]
        if y >= size_y:
            return yhi[z, y - size_y, c]
        return own[z, y, c]

    result = jnp.zeros((4 * columns, wide), jnp.float32)
    for z in range(size_z):
        for first in range(0, size_y, 2):
            span = range(first, min(first + 2, size_y))
            for y in span:
                for start in range(0, wide, 8):
                    c = pl.ds(start, 8)
                    total = base[z, y, c] + edge[z, y, c]
                    for distance, weight in enumerate(LAP_COEFFS, start=1):
                        beside = (at_z(z - distance, y, c) + at_z(z + distance, y, c)) + (
                            at_y(z, y - distance, c) + at_y(z, y + distance, c)
                        )
                        total = total + np.float32(-0.5 * weight) * beside
                    out[z, y, c] = total
            left = jnp.concatenate(
                [jnp.concatenate([own[z, y], xt[z, y], pt[z, y]], axis=0) for y in span], axis=1
            )
            right = jnp.concatenate([out[z, y] for y in span], axis=1)
            result = result + over_last(left, right)
    table[...] = result


def place_rows(meta, near, rows, slot, slots):
    size_x = rows.shape[1]
    per = 128 // BX
    start_x = meta[slot, 2]
    box = near[slot // slots, pl.ds(pl.multiple_of((slot % slots) * 8, 8), 8), :]
    lane = lax.broadcasted_iota(jnp.int32, box.shape, 1)
    gap = lane - start_x
    inside = (gap >= 0) & (gap < BX)
    for k in range(per):
        shift = lax.rem(start_x - k * BX + 2 * size_x, size_x)
        rows[k * 8 : (k + 1) * 8, :] = jnp.where(inside, pltpu.roll(box, shift, 1), 0.0)


def row_of(p, a, b):
    at = (p * BZ + a) * BY + b
    per = 128 // BX
    return (at % per) * 8 + at // per


def overlap_body(meta, near, fields, xt, pt, out, padded, rows, *, n_proj, slots):
    size_z, size_y, wide = fields.shape[0], fields.shape[1], fields.shape[2]
    columns = wide // 2
    padded[...] = jnp.zeros(padded.shape, jnp.float32)
    zs, ys = slice(BZ - 1, BZ - 1 + size_z), slice(BY - 1, BY - 1 + size_y)
    padded[zs, ys, :wide] = fields[...]
    padded[zs, ys, wide : wide + columns] = xt[...]
    padded[zs, ys, wide + columns :] = pt[...]
    out[...] = jnp.zeros(out.shape, jnp.float32)
    lane = lax.broadcasted_iota(jnp.int32, out.shape[1:], 1)
    per_tile = out.shape[2] // n_proj

    def step(slot, carry):
        @pl.when(meta[slot, 3] > 0)
        def _():
            place_rows(meta, near, rows, slot, slots)
            first_z = meta[slot, 0] + (BZ - 1)
            first_y = meta[slot, 1] + (BY - 1)
            sums = [jnp.zeros(out.shape[1:], jnp.float32) for _ in range(n_proj)]
            for a in range(BZ):
                for b in range(BY):
                    part = padded[first_z + a, first_y + b]
                    for p in range(n_proj):
                        row = row_of(p, a, b)
                        sums[p] = sums[p] + part * rows[row : row + 1, :]
            tile = slot // per_tile
            left = (slot % per_tile) * n_proj
            current = out[tile]
            for p in range(n_proj):
                current = jnp.where(
                    lane == left + p, jnp.sum(sums[p], axis=1, keepdims=True), current
                )
            out[tile] = current

        return carry

    lax.fori_loop(0, meta.shape[0], step, 0)


def finish_body(
    meta, near, back, total, fixed, fields, images, w_out, hw_out, gram, ray, padded, rows, coefs,
    *, n_proj, slots
):
    size_z, size_y, columns, size_x = w_out.shape
    c = columns
    full = total[...]
    grid = full[2 * c : 3 * c]
    which = lax.broadcasted_iota(jnp.int32, grid.shape, 0)
    for k in range(c):
        line = grid[k : k + 1, :]
        line = line * (1.0 / line[:, 2 * c + k : 2 * c + k + 1])
        grid = jnp.where(which == k, line, grid - grid[:, 2 * c + k : 2 * c + k + 1] * line)
    lane = lax.broadcasted_iota(jnp.int32, grid.shape, 1)
    theta = jnp.where(lane < c, pltpu.roll(grid, 128 - 4 * c, 1), 0.0)
    square = jnp.concatenate([theta, jnp.zeros((128 - c, 128), jnp.float32)], axis=0)
    turn = jnp.transpose(square)[:c, :c]

    def mix(value):
        return jnp.dot(turn, value, precision=HIGHEST, preferred_element_type=jnp.float32)

    left = jnp.concatenate([full[2 * c : 3 * c], full[c : 2 * c] - mix(full[:c]), full[3 * c :]], axis=0)
    nil = jnp.zeros((c, 128), jnp.float32)
    moved = jnp.concatenate(
        [pltpu.roll(theta, c, 1)] + [nil] * 5 + [pltpu.roll(theta, 5 * c, 1), nil], axis=0
    )
    tables = jnp.dot(
        left, fixed[...] - moved, precision=HIGHEST, preferred_element_type=jnp.float32
    )
    gram[...] = tables[:, : 3 * c]
    ray[...] = pltpu.roll(tables, 128 - 4 * c, 1)[:, : 3 * c]

    for t in range(back.shape[0]):
        coefs[t] = back[t, c:] - mix(back[t, :c])
    padded[...] = jnp.zeros(padded.shape, jnp.float32)
    per_tile = back.shape[2] // n_proj

    def step(slot, carry):
        @pl.when(meta[slot, 3] > 0)
        def _():
            place_rows(meta, near, rows, slot, slots)
            first_z = meta[slot, 0] + (BZ - 1)
            first_y = meta[slot, 1] + (BY - 1)
            tile = coefs[slot // per_tile]
            begin = (slot % per_tile) * n_proj
            scale = [
                jnp.sum(jnp.where(lane == begin + p, tile, 0.0), axis=1, keepdims=True)
                for p in range(n_proj)
            ]
            scale = [jnp.broadcast_to(s, (columns, size_x)) for s in scale]
            for a in range(BZ):
                for b in range(BY):
                    value = padded[first_z + a, first_y + b]
                    for p in range(n_proj):
                        row = row_of(p, a, b)
                        value = value + scale[p] * rows[row : row + 1, :]
                    padded[first_z + a, first_y + b] = value

        return carry

    lax.fori_loop(0, meta.shape[0], step, 0)
    for z in range(size_z):
        for y in range(size_y):
            mixed = mix(jnp.concatenate([fields[z, y, :c], images[z, y, :c]], axis=1))
            w_out[z, y] = fields[z, y, c:] - mixed[:, :size_x]
            hw_out[z, y] = images[z, y, c:] - mixed[:, size_x:] + padded[BZ - 1 + z, BY - 1 + y]


def per_device(
    block_x,
    block_hx,
    block_p,
    block_hp,
    potential,
    projectors,
    coupling,
    atom_count,
    proj_count,
    offsets,
    extents,
):
    columns, size_z, size_y, size_x = block_x.shape
    slots, n_proj = projectors.shape[-3], projectors.shape[-2]
    cells = size_z * size_y
    c, wide = columns, 2 * columns
    cell_weight = 1.0 / (
        cells * size_x * lax.axis_size("gx") * lax.axis_size("gy") * lax.axis_size("gz")
    )
    sym_coupling = (0.5 * (coupling + jnp.swapaxes(coupling, -1, -2)))[0, 0, 0]
    def add_lower(value, axis, dim, size):
        move = np.zeros((near.shape[1], 128), np.float32)
        move[slots * 8 :, dim] = size
        return jnp.concatenate([value, shifted(value, axis, 1) - move], axis=0)

    def turned(block):
        return jnp.transpose(block, (1, 2, 0, 3))

    xt, hxt, pt, hpt = turned(block_x), turned(block_hx), turned(block_p), turned(block_hp)
    inner, outer, pick_last, pick_first = band_matrices(size_x)
    fields, picked, near = kernel_call(
        functools.partial(prepare_body, slots=slots),
        9,
        [
            floats(size_z, size_y, wide, size_x),
            floats(16, cells * wide),
            floats(1, slots * 9, 128),
        ],
        scalars=4,
    )(
        offsets.reshape(3, slots),
        extents.reshape(3, slots),
        proj_count.reshape(slots),
        atom_count.reshape(1),
        projectors.reshape(slots, n_proj, -1),
        xt,
        hxt,
        potential,
        np.concatenate([pick_last, pick_first]),
    )
    zlo, zhi = both_sides(fields, "gz")
    ylo, yhi = both_sides(fields, "gy")
    near = add_lower(near, "gx", 2, size_x)
    sides = jnp.concatenate([shifted(picked[:8], "gx", 1), shifted(picked[8:], "gx", -1)], axis=0)
    near = add_lower(near, "gy", 1, size_y)
    base, early = kernel_call(
        early_body, 7, [floats(size_z, size_y, wide, size_x), floats(4 * c, 8 * c)]
    )(fields, xt, pt, hxt, hpt, potential, inner)
    base, early, near, sides = lax.optimization_barrier((base, early, near, sides))
    near = add_lower(near, "gz", 0, size_z)
    edge = lax.dot_general(sides, outer, (((0,), (0,)), ((), ())), precision=HIGHEST)
    edge = edge.reshape(fields.shape)
    facts = near[:, slots * 8 :, :8].reshape(-1, 8).astype(jnp.int32)
    reaches = jnp.all(facts[:, 0:3] + facts[:, 3:6] > 0, axis=1) & (facts[:, 6] > 0)
    meta = jnp.concatenate([facts[:, 0:3], reaches[:, None].astype(jnp.int32)], axis=1)

    pads = (size_z + 2 * BZ - 2, size_y + 2 * BY - 2)
    rows_shape = pltpu.VMEM((n_proj * BZ * BY, size_x), jnp.float32)
    tiles = meta.shape[0] * n_proj // 128
    found = kernel_call(
        functools.partial(overlap_body, n_proj=n_proj, slots=slots),
        5,
        floats(tiles, 4 * c, 128),
        [pltpu.VMEM(pads + (4 * c, size_x), jnp.float32), rows_shape],
        scalars=1,
    )(meta, near, fields, xt, pt)
    half = tiles // 2
    found = found[:half] + shifted(found[half:], "gz", -1)
    images, late = kernel_call(
        late_body, 9, [floats(size_z, size_y, wide, size_x), floats(4 * c, wide)]
    )(fields, zlo, zhi, ylo, yhi, base, edge, xt, pt)
    images, late, found = lax.optimization_barrier((images, late, found))
    found = found.transpose(1, 0, 2).reshape(4 * c, -1)
    half = found.shape[1] // 2
    found = found[:, :half] + shifted(found[:, half:], "gy", -1)
    half = found.shape[1] // 2
    found = found[:, :half] + shifted(found[:, half:], "gx", -1)
    eye = jnp.eye(slots, dtype=jnp.float32)
    spread_d = (eye[:, None, :, None] * sym_coupling[:, :, None, :]).reshape(
        slots * n_proj, slots * n_proj
    )
    weighted = jnp.dot(found[:wide], spread_d, precision=HIGHEST)
    late = late + over_last(found, weighted)
    total = early + jnp.pad(late, ((0, 0), (6 * c, 0)))
    total = all_sum(total, ("gz", "gy", "gx")) * cell_weight
    back = weighted
    for axis in ("gx", "gy"):
        back = jnp.concatenate([back, shifted(back, axis, 1)], axis=1)
    back = jnp.stack([back, shifted(back, "gz", 1)])
    back = back.reshape(2, wide, -1, 128).transpose(0, 2, 1, 3).reshape(-1, wide, 128)

    fixed = np.zeros((8 * c, 128), np.float32)
    one = np.eye(c, dtype=np.float32)
    for group, place in ((1, 1), (2, 0), (3, 2), (4, 4), (5, 6), (7, 5)):
        fixed[group * c : (group + 1) * c, place * c : (place + 1) * c] = one
    half_shape = floats(size_z, size_y, columns, size_x)
    w_t, hw_t, gram, rayleigh = kernel_call(
        functools.partial(finish_body, n_proj=n_proj, slots=slots),
        7,
        [half_shape, half_shape, floats(3 * c, 3 * c), floats(3 * c, 3 * c)],
        [
            pltpu.VMEM(pads + (columns, size_x), jnp.float32),
            rows_shape,
            pltpu.VMEM((tiles, columns, 128), jnp.float32),
        ],
        scalars=1,
    )(meta, near, back, total, fixed, fields, images)
    w_block = jnp.transpose(w_t, (2, 0, 1, 3))
    hw_block = jnp.transpose(hw_t, (2, 0, 1, 3))
    return (w_block, hw_block, gram, rayleigh)


def solution(mesh):
    in_specs = (
        P(None, "gz", "gy", "gx"),
        P(None, "gz", "gy", "gx"),
        P(None, "gz", "gy", "gx"),
        P(None, "gz", "gy", "gx"),
        P("gz", "gy", "gx"),
        P("gz", "gy", "gx", None, None, None),
        P("gz", "gy", "gx", None, None, None),
        P("gz", "gy", "gx"),
        P("gz", "gy", "gx", None),
        P(None, "gz", "gy", "gx", None),
        P(None, "gz", "gy", "gx", None),
    )
    out_specs = (P(None, "gz", "gy", "gx"), P(None, "gz", "gy", "gx"), P(), P())
    return jax.shard_map(
        per_device, mesh=mesh, in_specs=in_specs, out_specs=out_specs, check_vma=False
    )
```
